32 devices in a mesh: wide: 8 (over y, x, core), narrow: 4 (over z).
Axes of the slice: x: 2, y: 2, z: 4, core: 2. Of those that a mesh axis runs over, the one named last changes fastest.
Arguments:
- source_features: float32 [50, 16384], P(None, ('wide', 'narrow')), may hold values from -24 to 24
- target_features: float32 [50, 65536], P(None, 'narrow'), may hold values from -24 to 24
- source_mass: float32 [16384], P('wide'), may hold values from 0.05 to 20
- target_mass: float32 [65536], P('narrow'), may hold values from 0.05 to 20
- block_cols: int32 [128, 32], P('wide', 'narrow'), may hold values from 0 to 127, as said below
- block_counts: int32 [128, 4], P('wide', 'narrow'), may hold values from 1 to 8, as said below
Outputs:
- row_potential: float32 [16384], P('wide')
- col_potential: float32 [65536], P('narrow')
The draws below stay inside these ranges and needn't reach their ends.
Inputs may be any that keep to these rules, and one draw needn't show every extreme that they name: `block_cols`: each list of 8 entries holds distinct column tile ids of its group; every column tile of every group is the first entry of some row tile's list. `block_counts`: on the 16 row tiles of one index of wide and one column group the counts sum to at most 96, and to exactly 96 on some such device.
All inputs are finite; a program needn't handle non-finite values.
Results may differ from the reference program's by a relative error of at most 0.0003.
Values sent between devices are 32-bit elements; how exact they have to be, the bound alone decides.
A program may use at most 64 MiB of HBM per device.

```python
import math
import jax
import jax.numpy as jnp
from jax import lax

F = 50
TILE = 128
RT_DEV = 16
CT_DEV = 128
K_MAX = 8
ITERS = 2
ROW_GROUPS = 8
COL_GROUPS = 4
ROW_TILES = 128
ROWS = 16384
COLS = 65536
LIVE_MAX = 96


def draw_source_features(key, part):
    values = jnp.clip(jax.random.normal(key, (F, ROWS), jnp.float32), -6.0, 6.0)
    return values


def draw_target_features(key, part):
    values = jnp.clip(jax.random.normal(jax.random.fold_in(key, 3), (F, COLS), jnp.float32), -6.0, 6.0)
    return values


def draw_block_counts(key, part):
    key_total, key_heavy, key_units, key_tiles = jax.random.split(jax.random.fold_in(key, 21), 4)
    device_count = ROW_GROUPS * COL_GROUPS
    upper = max(RT_DEV, RT_DEV * K_MAX // 4)
    totals = jax.random.randint(key_total, (device_count,), RT_DEV, upper + 1)
    heaviest = jax.random.randint(key_heavy, (), 0, device_count)
    unit_count = RT_DEV * (K_MAX - 1)
    subkeys = jax.random.split(key_units, device_count)
    shuffled = jax.vmap(lambda subkey: jax.random.permutation(subkey, unit_count))(subkeys)
    needed = totals - RT_DEV
    chosen = jnp.arange(unit_count, dtype=jnp.int32)[None, :] < needed[:, None]
    owner = shuffled // (K_MAX - 1)
    belongs = (owner[:, :, None] == jnp.arange(RT_DEV, dtype=jnp.int32)[None, None, :]) & chosen[:, :, None]
    extras = jnp.sum(belongs.astype(jnp.int32), axis=1)
    tile_order = jax.random.permutation(key_tiles, RT_DEV)
    sequential = jnp.clip(LIVE_MAX - RT_DEV - tile_order * (K_MAX - 1), 0, K_MAX - 1)
    is_heavy = (jnp.arange(device_count, dtype=jnp.int32) == heaviest)[:, None]
    extras = jnp.where(is_heavy, sequential[None, :], extras)
    counts = 1 + extras
    counts = counts.reshape(ROW_GROUPS, COL_GROUPS, RT_DEV).transpose(0, 2, 1).reshape(ROW_TILES, COL_GROUPS)
    return counts.astype(jnp.int32)


def draw_block_cols(key, part):
    key_cover, key_others = jax.random.split(jax.random.fold_in(key, 33), 2)
    cover_keys = jax.random.split(key_cover, COL_GROUPS)
    coverage = jax.vmap(lambda subkey: jax.random.permutation(subkey, CT_DEV))(cover_keys)
    leading = coverage[:, jnp.arange(ROW_TILES, dtype=jnp.int32) % CT_DEV].T
    other_keys = jax.random.split(key_others, ROW_TILES * COL_GROUPS)
    others = jax.vmap(lambda subkey: jax.random.permutation(subkey, CT_DEV - 1)[:K_MAX - 1])(other_keys)
    others = others.reshape(ROW_TILES, COL_GROUPS, K_MAX - 1)
    following = (leading[:, :, None] + 1 + others) % CT_DEV
    lists = jnp.concatenate([leading[:, :, None], following], axis=2).reshape(ROW_TILES, COL_GROUPS * K_MAX)
    return lists.astype(jnp.int32)


def shard_levels(key, extent, cuts, low, largest):
    def one(position, blocks):
        heights = jax.random.uniform(jax.random.fold_in(jax.random.fold_in(key, 6), position), (blocks,), jnp.float32, low / len(cuts), largest / len(cuts))
        return jnp.repeat(jnp.exp(heights), extent[position] // blocks).reshape((-1,) + (1,) * (len(extent) - position - 1))

    factor_of = one(*cuts[0])
    for cut in cuts[1:]:
        factor_of = factor_of * one(*cut)
    return factor_of


def setup_inputs(seed: int = 0) -> dict:
    arg_keys = jax.random.split(jax.random.key(seed), 7)
    return {
        "source_features": draw_source_features(jax.random.fold_in(arg_keys[6], 71), 0),
        "target_features": draw_target_features(jax.random.fold_in(arg_keys[6], 71), 0),
        "source_mass": jnp.clip(jnp.exp(math.log(20.0) - 5.9914645 * jax.random.uniform(arg_keys[2], (ROWS,), jnp.float32) ** shard_levels(arg_keys[2], (ROWS,), ((0, 8),), -0.2, 0.2)), 0.05, 20.0),
        "target_mass": jnp.clip(jnp.exp(math.log(20.0) - 5.9914645 * jax.random.uniform(arg_keys[3], (COLS,), jnp.float32) ** shard_levels(arg_keys[3], (COLS,), ((0, 4),), -0.2, 0.2)), 0.05, 20.0),
        "block_cols": draw_block_cols(jax.random.fold_in(arg_keys[6], 71), 0),
        "block_counts": draw_block_counts(jax.random.fold_in(arg_keys[6], 71), 0),
    }


epsilon = 0.05
very_low = -1e30


def reference(source_features, target_features, source_mass, target_mass, block_cols, block_counts):
    col_total = COL_GROUPS * CT_DEV
    source_norm = jnp.sum(source_features * source_features, axis=0)
    target_norm = jnp.sum(target_features * target_features, axis=0)
    source_tiles = source_features.reshape(F, ROW_TILES, TILE)
    target_tiles = target_features.reshape(F, col_total, TILE)
    source_norm_tiles = source_norm.reshape(ROW_TILES, TILE)
    target_norm_tiles = target_norm.reshape(col_total, TILE)
    group_base = (jnp.arange(COL_GROUPS, dtype=jnp.int32) * CT_DEV)[None, :, None]
    global_cols = (block_cols.reshape(ROW_TILES, COL_GROUPS, K_MAX).astype(jnp.int32) + group_base).reshape(ROW_TILES, COL_GROUPS * K_MAX).astype(jnp.int32)
    is_live = (jnp.arange(K_MAX, dtype=jnp.int32)[None, None, :] < block_counts[:, :, None]).reshape(ROW_TILES, COL_GROUPS * K_MAX)

    def cost_tiles(row_tile):
        columns = global_cols[row_tile]
        source_part = source_tiles[:, row_tile, :]
        target_part = jnp.take(target_tiles, columns, axis=1)
        inner = jnp.einsum('fa,fsb->sab', source_part, target_part, precision=lax.Precision.HIGHEST)
        cost_tile = (source_norm_tiles[row_tile][None, :, None] + target_norm_tiles[columns][:, None, :] - 2.0 * inner) / F
        return cost_tile, columns, is_live[row_tile]

    def row_update(col_values):
        col_tiles = col_values.reshape(col_total, TILE)

        def one_tile(row_tile):
            cost_tile, columns, alive = cost_tiles(row_tile)
            scores = (col_tiles[columns][:, None, :] - cost_tile) / epsilon
            scores = jnp.where(alive[:, None, None], scores, very_low)
            highest = jnp.max(scores, axis=(0, 2))
            summed = jnp.sum(jnp.where(alive[:, None, None], jnp.exp(scores - highest[None, :, None]), 0.0), axis=(0, 2))
            return highest + jnp.log(summed)

        totals = lax.map(one_tile, jnp.arange(ROW_TILES, dtype=jnp.int32)).reshape(-1)
        return epsilon * jnp.log(source_mass) - epsilon * totals

    def col_update(row_values):
        row_tiles = row_values.reshape(ROW_TILES, TILE)

        def one_tile(running, row_tile):
            highest, summed = running
            cost_tile, columns, alive = cost_tiles(row_tile)
            scores = (row_tiles[row_tile][None, :, None] - cost_tile) / epsilon
            peaks = jnp.max(scores, axis=1)
            masses = jnp.sum(jnp.exp(scores - peaks[:, None, :]), axis=1)
            old_high = highest[columns]
            old_sum = summed[columns]
            new_high = jnp.maximum(old_high, peaks)
            new_sum = old_sum * jnp.exp(old_high - new_high) + masses * jnp.exp(peaks - new_high)
            target_index = jnp.where(alive, columns, col_total).astype(jnp.int32)
            highest = highest.at[target_index].set(new_high, mode='drop')
            summed = summed.at[target_index].set(new_sum, mode='drop')
            return (highest, summed), None

        initial = (jnp.full((col_total, TILE), very_low, jnp.float32), jnp.zeros((col_total, TILE), jnp.float32))
        (highest, summed), _ = lax.scan(one_tile, initial, jnp.arange(ROW_TILES, dtype=jnp.int32))
        return epsilon * jnp.log(target_mass) - epsilon * (highest.reshape(-1) + jnp.log(summed.reshape(-1)))

    col_values = jnp.zeros((col_total * TILE,), jnp.float32)
    row_values = jnp.zeros((ROW_TILES * TILE,), jnp.float32)
    for iteration in range(ITERS):
        row_values = row_update(col_values)
        col_values = col_update(row_values)
    return row_values, col_values
```

```python
import functools

import jax
import jax.numpy as jnp
from jax import lax
from jax.experimental import pallas as pl
from jax.experimental.pallas import tpu as pltpu
from jax.sharding import PartitionSpec as P

F = 50
TILE = 128
K_MAX = 8
ITERS = 2
PAD = 64

epsilon = 0.05
very_low = -1e30
product_scale = 2.0 / (F * epsilon)
norm_scale = 1.0 / (F * epsilon)


def split_three(x):
    first = x.astype(jnp.bfloat16)
    rest = x - first.astype(jnp.float32)
    second = rest.astype(jnp.bfloat16)
    third = (rest - second.astype(jnp.float32)).astype(jnp.bfloat16)
    return first, second, third


def padded(x):
    return jnp.concatenate([x, jnp.zeros((PAD - F, TILE), jnp.float32)], axis=0)


def kernel(
    wide_size,
    narrow_size,
    cols_ref,
    counts_ref,
    source_ref,
    target_ref,
    row_mass_ref,
    col_mass_ref,
    row_out_ref,
    col_out_ref,
    gathered,
    left,
    right,
    scores,
    one_hot,
    source_norm,
    target_norm,
    col_values,
    col_pieces,
    row_send,
    row_recv,
    slot_peak,
    slot_mass,
    col_peak,
    col_send,
    col_recv,
    gather_send_sem,
    gather_recv_sem,
    row_send_sem,
    row_recv_sem,
    scatter_send_sem,
    scatter_recv_sem,
    spread_send_sem,
    spread_recv_sem,
):
    wide = lax.axis_index("wide")
    narrow = lax.axis_index("narrow")
    row_count = cols_ref.shape[0]
    col_count = col_mass_ref.shape[0]
    shard_tiles = row_count // narrow_size
    piece = col_count // wide_size

    def wide_peer(d):
        return lax.rem(wide + d, wide_size)

    def narrow_peer(d):
        return lax.rem(narrow + d, narrow_size)

    def at_wide(w):
        return {"wide": w, "narrow": narrow}

    def at_narrow(z):
        return {"wide": wide, "narrow": z}

    def remote(src, dst, send, recv, where):
        return pltpu.make_async_remote_copy(
            src_ref=src,
            dst_ref=dst,
            send_sem=send,
            recv_sem=recv,
            device_id=where,
            device_id_type=pl.DeviceIdType.MESH,
        )

    barrier = pltpu.get_barrier_semaphore()
    for d in range(1, narrow_size):
        pl.semaphore_signal(
            barrier, inc=1, device_id=at_narrow(narrow_peer(d)), device_id_type=pl.DeviceIdType.MESH
        )
    for d in range(1, wide_size):
        pl.semaphore_signal(
            barrier, inc=1, device_id=at_wide(wide_peer(d)), device_id_type=pl.DeviceIdType.MESH
        )
    pl.semaphore_wait(barrier, narrow_size + wide_size - 2)

    def exchange(axis_size, peer, where, src_of, buffer, me, send_sem, recv_sem):
        sends = []
        for d in range(1, axis_size):
            to = peer(d)
            copy = remote(
                src_of(to), buffer.at[me], send_sem.at[d - 1], recv_sem.at[d - 1], where(to)
            )
            copy.start()
            sends.append(copy)

        def finish():
            for d in range(1, axis_size):
                origin = lax.rem(me + axis_size - d, axis_size)
                remote(
                    src_of(peer(d)),
                    buffer.at[origin],
                    send_sem.at[d - 1],
                    recv_sem.at[d - 1],
                    where(peer(d)),
                ).wait_recv()
            for copy in sends:
                copy.wait_send()

        return finish

    finish_gather = exchange(
        narrow_size,
        narrow_peer,
        at_narrow,
        lambda to: source_ref,
        gathered,
        narrow,
        gather_send_sem,
        gather_recv_sem,
    )
    gathered[narrow] = source_ref[...]

    def prepare_target(c, carry):
        x = padded(target_ref[:, pl.ds(pl.multiple_of(c * TILE, TILE), TILE)])
        first, second, third = split_three(x)
        right[c, 0:PAD, :] = first
        right[c, PAD : 2 * PAD, :] = second
        right[c, 2 * PAD : 3 * PAD, :] = third
        norm = jnp.sum(x * x, axis=0, keepdims=True) * norm_scale
        target_norm[pl.ds(c, 1), :] = norm
        return carry

    lax.fori_loop(0, col_count, prepare_target, 0)
    col_values[...] = -target_norm[...]
    finish_gather()

    lane = lax.broadcasted_iota(jnp.int32, (1, TILE), 1)

    def prepare_source(z, carry):
        for t in range(shard_tiles):
            r = z * shard_tiles + t
            x = padded(gathered[z, :, t * TILE : (t + 1) * TILE])
            source_norm[pl.ds(r, 1), :] = jnp.sum(x * x, axis=0, keepdims=True) * norm_scale
            first, second, third = split_three(x * product_scale)
            first, second, third = [p.astype(jnp.float32) for p in (first, second, third)]
            stacked = jnp.concatenate([first, first, first, second, second, third], axis=0)
            left[r] = jnp.transpose(stacked).astype(jnp.bfloat16)
        return carry

    lax.fori_loop(0, narrow_size, prepare_source, 0)

    def multiply(r, carry):
        a = left[r]
        marks = []
        for k in range(K_MAX):
            c = cols_ref[r, k]
            alive = k < counts_ref[r, 0]
            b = right[c]
            b = jnp.concatenate([b, b[0 : 2 * PAD], b[0:PAD]], axis=0)
            product = jnp.dot(a, b, preferred_element_type=jnp.float32)
            scores[r * K_MAX + k] = jnp.where(alive, product, very_low)
            marks.append((lane == jnp.where(alive, c, -1)).astype(jnp.float32))
        one_hot[pl.ds(pl.multiple_of(r * K_MAX, K_MAX), K_MAX), :] = jnp.concatenate(marks, axis=0)
        return carry

    lax.fori_loop(0, row_count, multiply, 0)

    half = TILE // 2
    row_lane = lax.broadcasted_iota(jnp.int32, (TILE, TILE), 1)

    def row_pass(step):
        def one_tile(r, carry):
            peaks, masses = carry
            tile_peaks, tile_masses = [], []
            values = [col_values[pl.ds(cols_ref[r, k], 1), :] for k in range(K_MAX)]
            for h in range(2):
                rows = slice(h * half, (h + 1) * half)
                top = None
                for k in range(K_MAX):
                    s = scores[r * K_MAX + k, rows, :] + values[k]
                    top = s if top is None else jnp.maximum(top, s)
                top = jnp.max(top, axis=1, keepdims=True)
                total = None
                for k in range(K_MAX):
                    s = jnp.exp(scores[r * K_MAX + k, rows, :] + values[k] - top)
                    total = s if total is None else total + s
                tile_peaks.append(top)
                tile_masses.append(jnp.sum(total, axis=1, keepdims=True))
            here = row_lane == r
            peaks = jnp.where(here, jnp.concatenate(tile_peaks, axis=0), peaks)
            masses = jnp.where(here, jnp.concatenate(tile_masses, axis=0), masses)
            return peaks, masses

        zero = jnp.zeros((TILE, TILE), jnp.float32)
        peaks, masses = lax.fori_loop(0, row_count, one_tile, (zero, zero))
        row_send[step, 0:row_count, :] = jnp.transpose(peaks)[0:row_count]
        row_send[step, row_count : 2 * row_count, :] = jnp.transpose(masses)[0:row_count]
        finish = exchange(
            narrow_size,
            narrow_peer,
            at_narrow,
            lambda to: row_send.at[step],
            row_recv.at[step],
            narrow,
            row_send_sem.at[step],
            row_recv_sem.at[step],
        )
        row_recv[step, narrow] = row_send[step]
        finish()
        parts = [row_recv[step, z] for z in range(narrow_size)]
        top = functools.reduce(jnp.maximum, [p[0:row_count] for p in parts])
        total = sum(p[row_count:] * jnp.exp(p[0:row_count] - top) for p in parts)
        return jnp.log(row_mass_ref[...]) - (top + jnp.log(total))

    col_index = lax.broadcasted_iota(jnp.int32, (col_count, TILE), 0)

    def col_pass(step, row_values_ref):
        def one_tile(r, highest):
            values = jnp.transpose(
                jnp.broadcast_to(row_values_ref[pl.ds(r, 1), :], (TILE, TILE))
            )
            peaks, masses = [], []
            for k in range(K_MAX):
                alive = k < counts_ref[r, 0]
                s = scores[r * K_MAX + k] + values
                top = jnp.max(s, axis=0, keepdims=True)
                total = jnp.sum(jnp.exp(s - top), axis=0, keepdims=True)
                top = jnp.where(alive, top, very_low)
                highest = jnp.where(
                    col_index == cols_ref[r, k], jnp.maximum(highest, top), highest
                )
                peaks.append(top)
                masses.append(jnp.where(alive, total, 0.0))
            place = pl.ds(pl.multiple_of(r * K_MAX, K_MAX), K_MAX)
            slot_peak[place, :] = jnp.concatenate(peaks, axis=0)
            slot_mass[place, :] = jnp.concatenate(masses, axis=0)
            return highest

        highest = lax.fori_loop(
            0, row_count, one_tile, jnp.full((col_count, TILE), very_low, jnp.float32)
        )
        col_peak[...] = highest

        def rescale(r, carry):
            place = pl.ds(pl.multiple_of(r * K_MAX, K_MAX), K_MAX)
            tops = jnp.concatenate(
                [col_peak[pl.ds(cols_ref[r, k], 1), :] for k in range(K_MAX)], axis=0
            )
            slot_mass[place, :] = slot_mass[place, :] * jnp.exp(
                jnp.minimum(slot_peak[place, :] - tops, 0.0)
            )
            return carry

        lax.fori_loop(0, row_count, rescale, 0)
        summed = lax.dot_general(
            one_hot[...],
            slot_mass[...],
            (((0,), (0,)), ((), ())),
            precision=lax.Precision.HIGHEST,
            preferred_element_type=jnp.float32,
        )
        for w in range(wide_size):
            col_send[step, w, 0] = highest[w * piece : (w + 1) * piece]
            col_send[step, w, 1] = summed[w * piece : (w + 1) * piece]
        finish = exchange(
            wide_size,
            wide_peer,
            at_wide,
            lambda to: col_send.at[step, to],
            col_recv.at[step],
            wide,
            scatter_send_sem.at[step],
            scatter_recv_sem.at[step],
        )
        col_recv[step, wide] = col_send[step, wide]
        finish()
        parts = [col_recv[step, w] for w in range(wide_size)]
        top = functools.reduce(jnp.maximum, [p[0] for p in parts])
        total = sum(p[1] * jnp.exp(p[0] - top) for p in parts)
        mass = col_mass_ref[pl.ds(pl.multiple_of(wide * piece, piece), piece), :]
        col_pieces[step, wide] = jnp.log(mass) - (top + jnp.log(total))
        finish = exchange(
            wide_size,
            wide_peer,
            at_wide,
            lambda to: col_pieces.at[step, wide],
            col_pieces.at[step],
            wide,
            spread_send_sem.at[step],
            spread_recv_sem.at[step],
        )
        finish()
        for w in range(wide_size):
            col_values[w * piece : (w + 1) * piece, :] = col_pieces[step, w]

    for step in range(ITERS):
        row_out_ref[...] = row_pass(step)
        col_pass(step, row_out_ref)
    row_out_ref[...] = epsilon * (row_out_ref[...] + source_norm[...])
    col_out_ref[...] = epsilon * (col_values[...] + target_norm[...])


def local(
    wide_size,
    narrow_size,
    source_features,
    target_features,
    source_mass,
    target_mass,
    block_cols,
    block_counts,
):
    row_count = source_mass.shape[0] // TILE
    col_count = target_mass.shape[0] // TILE
    slots = row_count * K_MAX
    piece = col_count // wide_size
    vmem = pl.BlockSpec(memory_space=pltpu.VMEM)
    smem = pl.BlockSpec(memory_space=pltpu.SMEM)
    f32 = jnp.float32
    dma = pltpu.SemaphoreType.DMA
    rows, cols = pl.pallas_call(
        functools.partial(kernel, wide_size, narrow_size),
        out_shape=(
            jax.ShapeDtypeStruct((row_count, TILE), f32),
            jax.ShapeDtypeStruct((col_count, TILE), f32),
        ),
        in_specs=[smem, smem, vmem, vmem, vmem, vmem],
        out_specs=(vmem, vmem),
        scratch_shapes=[
            pltpu.VMEM((narrow_size, F, source_features.shape[1]), f32),
            pltpu.VMEM((row_count, TILE, 6 * PAD), jnp.bfloat16),
            pltpu.VMEM((col_count, 3 * PAD, TILE), jnp.bfloat16),
            pltpu.VMEM((slots, TILE, TILE), f32),
            pltpu.VMEM((slots, col_count), f32),
            pltpu.VMEM((row_count, TILE), f32),
            pltpu.VMEM((col_count, TILE), f32),
            pltpu.VMEM((col_count, TILE), f32),
            pltpu.VMEM((ITERS, wide_size, piece, TILE), f32),
            pltpu.VMEM((ITERS, 2 * row_count, TILE), f32),
            pltpu.VMEM((ITERS, narrow_size, 2 * row_count, TILE), f32),
            pltpu.VMEM((slots, TILE), f32),
            pltpu.VMEM((slots, TILE), f32),
            pltpu.VMEM((col_count, TILE), f32),
            pltpu.VMEM((ITERS, wide_size, 2, piece, TILE), f32),
            pltpu.VMEM((ITERS, wide_size, 2, piece, TILE), f32),
            dma((narrow_size - 1,)),
            dma((narrow_size - 1,)),
            dma((ITERS, narrow_size - 1)),
            dma((ITERS, narrow_size - 1)),
            dma((ITERS, wide_size - 1)),
            dma((ITERS, wide_size - 1)),
            dma((ITERS, wide_size - 1)),
            dma((ITERS, wide_size - 1)),
        ],
        compiler_params=pltpu.CompilerParams(
            collective_id=0, has_side_effects=True, vmem_limit_bytes=50 << 20
        ),
    )(
        block_cols,
        block_counts,
        source_features,
        target_features,
        source_mass.reshape(row_count, TILE),
        target_mass.reshape(col_count, TILE),
    )
    return rows.reshape(-1), cols.reshape(-1)


def solution(mesh):
    in_specs = (
        P(None, ("wide", "narrow")),
        P(None, "narrow"),
        P("wide"),
        P("narrow"),
        P("wide", "narrow"),
        P("wide", "narrow"),
    )
    out_specs = (P("wide"), P("narrow"))
    return jax.shard_map(
        functools.partial(local, mesh.shape["wide"], mesh.shape["narrow"]),
        mesh=mesh,
        in_specs=in_specs,
        out_specs=out_specs,
        check_vma=False,
    )
```

```python
import functools

import jax
import jax.numpy as jnp
from jax import lax
from jax.experimental import pallas as pl
from jax.experimental.pallas import tpu as pltpu
from jax.sharding import PartitionSpec as P

F = 50
TILE = 128
K_MAX = 8
ITERS = 2
PAD = 64
CHUNKS = 4

epsilon = 0.05
very_low = -1e30
log2_e = 1.4426950408889634
product_scale = 2.0 * log2_e / (F * epsilon)
norm_scale = log2_e / (F * epsilon)
potential_scale = epsilon / log2_e


def split_three(x):
    first = x.astype(jnp.bfloat16)
    rest = x - first.astype(jnp.float32)
    second = rest.astype(jnp.bfloat16)
    third = (rest - second.astype(jnp.float32)).astype(jnp.bfloat16)
    return first, second, third


def log2(x):
    return jnp.log(x) * log2_e


def padded(x):
    return jnp.concatenate([x, jnp.zeros((PAD - F, TILE), jnp.float32)], axis=0)


def kernel(
    wide_size,
    narrow_size,
    cols_ref,
    counts_ref,
    source_hbm,
    target_hbm,
    row_mass_hbm,
    col_mass_hbm,
    row_out_ref,
    col_out_ref,
    gathered,
    target_ref,
    row_mass_ref,
    col_mass_ref,
    right,
    scores,
    one_hot,
    marked,
    source_norm,
    target_norm,
    col_values,
    col_pieces,
    row_columns,
    row_send,
    row_recv,
    slot_lse,
    slot_mass,
    col_peak,
    col_send,
    col_recv,
    load_sem,
    gather_send_sem,
    gather_recv_sem,
    row_send_sem,
    row_recv_sem,
    scatter_send_sem,
    scatter_recv_sem,
    spread_send_sem,
    spread_recv_sem,
):
    wide = lax.axis_index("wide")
    narrow = lax.axis_index("narrow")
    row_count = row_mass_ref.shape[0]
    col_count = col_mass_ref.shape[0]
    shard_tiles = row_count // narrow_size
    piece = col_count // wide_size
    chunk_tiles = col_count // CHUNKS
    chunk_cols = chunk_tiles * TILE

    def wide_peer(d):
        return lax.rem(wide + d, wide_size)

    def narrow_peer(d):
        return lax.rem(narrow + d, narrow_size)

    def at_wide(w):
        return {"wide": w, "narrow": narrow}

    def at_narrow(z):
        return {"wide": wide, "narrow": z}

    def remote(src, dst, send, recv, where):
        return pltpu.make_async_remote_copy(
            src_ref=src,
            dst_ref=dst,
            send_sem=send,
            recv_sem=recv,
            device_id=where,
            device_id_type=pl.DeviceIdType.MESH,
        )

    barrier = pltpu.get_barrier_semaphore()
    for d in range(1, narrow_size):
        pl.semaphore_signal(
            barrier, inc=1, device_id=at_narrow(narrow_peer(d)), device_id_type=pl.DeviceIdType.MESH
        )
    for d in range(1, wide_size):
        pl.semaphore_signal(
            barrier, inc=1, device_id=at_wide(wide_peer(d)), device_id_type=pl.DeviceIdType.MESH
        )
    loads = [pltpu.make_async_copy(source_hbm, gathered.at[narrow], load_sem.at[CHUNKS])]
    for q in range(CHUNKS):
        part = pl.ds(q * chunk_cols, chunk_cols)
        loads.append(
            pltpu.make_async_copy(target_hbm.at[:, part], target_ref.at[:, part], load_sem.at[q])
        )
    loads.append(pltpu.make_async_copy(row_mass_hbm, row_mass_ref, load_sem.at[CHUNKS + 1]))
    loads.append(pltpu.make_async_copy(col_mass_hbm, col_mass_ref, load_sem.at[CHUNKS + 2]))
    for load in loads:
        load.start()
    pl.semaphore_wait(barrier, narrow_size + wide_size - 2)

    def exchange(axis_size, peer, where, src_of, buffer, me, send_sem, recv_sem):
        sends = []
        for d in range(1, axis_size):
            to = peer(d)
            copy = remote(
                src_of(to), buffer.at[me], send_sem.at[d - 1], recv_sem.at[d - 1], where(to)
            )
            copy.start()
            sends.append(copy)

        def arrive(d):
            origin = lax.rem(me + axis_size - d, axis_size)
            remote(
                src_of(peer(d)),
                buffer.at[origin],
                send_sem.at[d - 1],
                recv_sem.at[d - 1],
                where(peer(d)),
            ).wait_recv()

        def leave():
            for copy in sends:
                copy.wait_send()

        def finish():
            for d in range(1, axis_size):
                arrive(d)
            leave()

        return finish, arrive, leave

    _, gather_arrive, gather_leave = exchange(
        narrow_size,
        narrow_peer,
        at_narrow,
        lambda to: source_hbm,
        gathered,
        narrow,
        gather_send_sem,
        gather_recv_sem,
    )

    def prepare_target(c, carry):
        x = padded(target_ref[:, pl.ds(pl.multiple_of(c * TILE, TILE), TILE)])
        first, second, third = split_three(x)
        right[c, 0:PAD, :] = first
        right[c, PAD : 2 * PAD, :] = second
        right[c, 2 * PAD : 3 * PAD, :] = third
        norm = jnp.sum(x * x, axis=0, keepdims=True) * norm_scale
        target_norm[pl.ds(c, 1), :] = norm
        return carry

    loads[0].wait()
    for q in range(CHUNKS):
        loads[q + 1].wait()
        lax.fori_loop(q * chunk_tiles, (q + 1) * chunk_tiles, prepare_target, 0)
    col_values[...] = -target_norm[...]
    loads[CHUNKS + 1].wait()
    loads[CHUNKS + 2].wait()

    lane = lax.broadcasted_iota(jnp.int32, (1, TILE), 1)
    row_lane = lax.broadcasted_iota(jnp.int32, (TILE, TILE), 1)
    slab = 8

    def row_tile(r):
        values = [col_values[pl.ds(cols_ref[k, r], 1), :] for k in range(K_MAX)]
        tops, totals = [], []
        for h in range(TILE // slab):
            rows = slice(h * slab, (h + 1) * slab)
            s = [scores[r * K_MAX + k, rows, :] + values[k] for k in range(K_MAX)]
            top = functools.reduce(jnp.maximum, s)
            totals.append(sum(jnp.exp2(x - top) for x in s))
            tops.append(top)
        top = jnp.concatenate(tops, axis=0)
        total = jnp.concatenate(totals, axis=0)
        peak = jnp.max(top, axis=1, keepdims=True)
        mass = jnp.sum(total * jnp.exp2(top - peak), axis=1, keepdims=True)
        row_columns[...] = jnp.where(
            row_lane == r,
            peak,
            jnp.where(row_lane == r + TILE // 2, mass, row_columns[...]),
        )

    def first_tile(r, x):
        source_norm[pl.ds(r, 1), :] = jnp.sum(x * x, axis=0, keepdims=True) * norm_scale
        first, second, third = split_three(x * product_scale)
        first, second, third = [p.astype(jnp.float32) for p in (first, second, third)]
        stacked = jnp.concatenate([first, first, first, second, second, third], axis=0)
        a = jnp.transpose(stacked).astype(jnp.bfloat16)
        marks = []
        for k in range(0, K_MAX, 2):
            pair = []
            for j in (k, k + 1):
                c = cols_ref[j, r]
                alive = j < counts_ref[0, r]
                b = right[c]
                pair.append(jnp.concatenate([b, b[0 : 2 * PAD], b[0:PAD]], axis=0))
                marks.append((lane == jnp.where(alive, c, -1)).astype(jnp.float32))
            product = jnp.dot(
                a, jnp.concatenate(pair, axis=1), preferred_element_type=jnp.float32
            )
            for j in (k, k + 1):
                alive = j < counts_ref[0, r]
                part = product[:, (j - k) * TILE : (j - k + 1) * TILE]
                scores[r * K_MAX + j] = jnp.where(alive, part, very_low)
        marks = jnp.concatenate(marks, axis=0)
        one_hot[pl.ds(pl.multiple_of(r * K_MAX, K_MAX), K_MAX), :] = marks
        unmarked = 1.0 - jnp.sum(marks, axis=0, keepdims=True)
        marked[r] = jnp.concatenate(
            [marks, marks, unmarked, jnp.zeros((2 * K_MAX - 1, TILE), jnp.float32)], axis=0
        ).astype(jnp.bfloat16)
        row_tile(r)

    row_columns[...] = jnp.zeros((TILE, TILE), jnp.float32)
    for d in range(narrow_size):
        if d > 0:
            gather_arrive(d)
        z = lax.rem(narrow + narrow_size - d, narrow_size)

        def one(t, carry):
            x = padded(gathered[z, :, pl.ds(pl.multiple_of(t * TILE, TILE), TILE)])
            first_tile(z * shard_tiles + t, x)
            return carry

        lax.fori_loop(0, shard_tiles, one, 0)
    gather_leave()

    def row_combine(step):
        columns = jnp.transpose(row_columns[...])
        half = TILE // 2
        row_send[step] = columns[0:row_count] + log2(columns[half : half + row_count])
        finish, _, _ = exchange(
            narrow_size,
            narrow_peer,
            at_narrow,
            lambda to: row_send.at[step],
            row_recv.at[step],
            narrow,
            row_send_sem.at[step],
            row_recv_sem.at[step],
        )
        row_recv[step, narrow] = row_send[step]
        finish()
        parts = [row_recv[step, z] for z in range(narrow_size)]
        top = functools.reduce(jnp.maximum, parts)
        total = sum(jnp.exp2(p - top) for p in parts)
        return log2(row_mass_ref[...]) - (top + log2(total))

    def col_pass(step, row_values_ref):
        def one_tile(r, carry):
            values = jnp.transpose(
                jnp.broadcast_to(row_values_ref[pl.ds(r, 1), :], (TILE, TILE))
            )
            results = []
            for k in range(K_MAX):
                s = [
                    scores[r * K_MAX + k, h * slab : (h + 1) * slab, :]
                    + values[h * slab : (h + 1) * slab]
                    for h in range(TILE // slab)
                ]
                top = functools.reduce(jnp.maximum, s)
                total = sum(jnp.exp2(x - top) for x in s)
                peak = jnp.max(top, axis=0, keepdims=True)
                mass = jnp.sum(total * jnp.exp2(top - peak), axis=0, keepdims=True)
                alive = k < counts_ref[0, r]
                results.append((jnp.where(alive, peak, very_low), mass))
            lse = jnp.concatenate([p for p, _ in results], axis=0) + log2(
                jnp.concatenate([m for _, m in results], axis=0)
            )
            slot_lse[pl.ds(pl.multiple_of(r * K_MAX, K_MAX), K_MAX), :] = lse
            coarse = lse.astype(jnp.bfloat16).astype(jnp.float32)
            stack = jnp.concatenate(
                [
                    coarse,
                    lse - coarse,
                    jnp.full((1, TILE), very_low, jnp.float32),
                    jnp.zeros((2 * K_MAX - 1, TILE), jnp.float32),
                ],
                axis=0,
            ).astype(jnp.bfloat16)
            spread = lax.dot_general(
                marked[r],
                stack,
                (((0,), (0,)), ((), ())),
                preferred_element_type=jnp.float32,
            )
            col_peak[...] = jnp.maximum(col_peak[...], spread)
            return carry

        col_peak[...] = jnp.full((col_count, TILE), very_low, jnp.float32)
        lax.fori_loop(0, row_count, one_tile, 0)

        def rescale(r, carry):
            place = pl.ds(pl.multiple_of(r * K_MAX, K_MAX), K_MAX)
            tops = jnp.concatenate(
                [col_peak[pl.ds(cols_ref[k, r], 1), :] for k in range(K_MAX)], axis=0
            )
            slot_mass[place, :] = jnp.exp2(jnp.minimum(slot_lse[place, :] - tops, 1e2))
            return carry

        lax.fori_loop(0, row_count, rescale, 0)
        summed = lax.dot_general(
            one_hot[...],
            slot_mass[...],
            (((0,), (0,)), ((), ())),
            precision=lax.Precision.HIGHEST,
            preferred_element_type=jnp.float32,
        )
        lse = jnp.where(
            summed > 0.0, col_peak[...] + log2(jnp.maximum(summed, 1e-30)), very_low
        )
        for w in range(wide_size):
            col_send[step, w] = lse[w * piece : (w + 1) * piece]
        finish, _, _ = exchange(
            wide_size,
            wide_peer,
            at_wide,
            lambda to: col_send.at[step, to],
            col_recv.at[step],
            wide,
            scatter_send_sem.at[step],
            scatter_recv_sem.at[step],
        )
        col_recv[step, wide] = col_send[step, wide]
        finish()
        parts = [col_recv[step, w] for w in range(wide_size)]
        top = functools.reduce(jnp.maximum, parts)
        total = sum(jnp.exp2(p - top) for p in parts)
        mass = col_mass_ref[pl.ds(pl.multiple_of(wide * piece, piece), piece), :]
        col_pieces[step, wide] = log2(mass) - (top + log2(total))
        finish, _, _ = exchange(
            wide_size,
            wide_peer,
            at_wide,
            lambda to: col_pieces.at[step, wide],
            col_pieces.at[step],
            wide,
            spread_send_sem.at[step],
            spread_recv_sem.at[step],
        )
        finish()
        for w in range(wide_size):
            col_values[w * piece : (w + 1) * piece, :] = col_pieces[step, w]

    def row_pass(r, carry):
        row_tile(r)
        return carry

    for step in range(ITERS):
        if step > 0:
            lax.fori_loop(0, row_count, row_pass, 0)
        row_out_ref[...] = row_combine(step)
        col_pass(step, row_out_ref)
    row_out_ref[...] = potential_scale * (row_out_ref[...] + source_norm[...])
    col_out_ref[...] = potential_scale * (col_values[...] + target_norm[...])


def local(
    wide_size,
    narrow_size,
    source_features,
    target_features,
    source_mass,
    target_mass,
    block_cols,
    block_counts,
):
    row_count = source_mass.shape[0] // TILE
    col_count = target_mass.shape[0] // TILE
    slots = row_count * K_MAX
    piece = col_count // wide_size
    vmem = pl.BlockSpec(memory_space=pltpu.VMEM)
    smem = pl.BlockSpec(memory_space=pltpu.SMEM)
    hbm = pl.BlockSpec(memory_space=pltpu.HBM)
    f32 = jnp.float32
    dma = pltpu.SemaphoreType.DMA
    rows, cols = pl.pallas_call(
        functools.partial(kernel, wide_size, narrow_size),
        out_shape=(
            jax.ShapeDtypeStruct((row_count, TILE), f32),
            jax.ShapeDtypeStruct((col_count, TILE), f32),
        ),
        in_specs=[smem, smem, hbm, hbm, hbm, hbm],
        out_specs=(vmem, vmem),
        scratch_shapes=[
            pltpu.VMEM((narrow_size, F, source_features.shape[1]), f32),
            pltpu.VMEM(target_features.shape, f32),
            pltpu.VMEM((row_count, TILE), f32),
            pltpu.VMEM((col_count, TILE), f32),
            pltpu.VMEM((col_count, 3 * PAD, TILE), jnp.bfloat16),
            pltpu.VMEM((slots, TILE, TILE), f32),
            pltpu.VMEM((slots, col_count), f32),
            pltpu.VMEM((row_count, 4 * K_MAX, col_count), jnp.bfloat16),
            pltpu.VMEM((row_count, TILE), f32),
            pltpu.VMEM((col_count, TILE), f32),
            pltpu.VMEM((col_count, TILE), f32),
            pltpu.VMEM((ITERS, wide_size, piece, TILE), f32),
            pltpu.VMEM((TILE, TILE), f32),
            pltpu.VMEM((ITERS, row_count, TILE), f32),
            pltpu.VMEM((ITERS, narrow_size, row_count, TILE), f32),
            pltpu.VMEM((slots, TILE), f32),
            pltpu.VMEM((slots, TILE), f32),
            pltpu.VMEM((col_count, TILE), f32),
            pltpu.VMEM((ITERS, wide_size, piece, TILE), f32),
            pltpu.VMEM((ITERS, wide_size, piece, TILE), f32),
            dma((CHUNKS + 3,)),
            dma((narrow_size - 1,)),
            dma((narrow_size - 1,)),
            dma((ITERS, narrow_size - 1)),
            dma((ITERS, narrow_size - 1)),
            dma((ITERS, wide_size - 1)),
            dma((ITERS, wide_size - 1)),
            dma((ITERS, wide_size - 1)),
            dma((ITERS, wide_size - 1)),
        ],
        compiler_params=pltpu.CompilerParams(
            collective_id=0, has_side_effects=True, vmem_limit_bytes=67043328
        ),
    )(
        block_cols.T,
        block_counts.T,
        source_features,
        target_features,
        source_mass.reshape(row_count, TILE),
        target_mass.reshape(col_count, TILE),
    )
    return rows.reshape(-1), cols.reshape(-1)


def solution(mesh):
    in_specs = (
        P(None, ("wide", "narrow")),
        P(None, "narrow"),
        P("wide"),
        P("narrow"),
        P("wide", "narrow"),
        P("wide", "narrow"),
    )
    out_specs = (P("wide"), P("narrow"))
    return jax.shard_map(
        functools.partial(local, mesh.shape["wide"], mesh.shape["narrow"]),
        mesh=mesh,
        in_specs=in_specs,
        out_specs=out_specs,
        check_vma=False,
    )
```

```python
import functools

import jax
import jax.numpy as jnp
from jax import lax
from jax.experimental import pallas as pl
from jax.experimental.pallas import tpu as pltpu
from jax.sharding import PartitionSpec as P

F = 50
TILE = 128
K_MAX = 8
ITERS = 2
PAD = 64
CHUNKS = 4
SLABS = 16
GROUP = 4

epsilon = 0.05
very_low = -1e30
log2_e = 1.4426950408889634
product_scale = 2.0 * log2_e / (F * epsilon)
norm_scale = log2_e / (F * epsilon)
potential_scale = epsilon / log2_e


def split_three(x):
    first = x.astype(jnp.bfloat16)
    rest = x - first.astype(jnp.float32)
    second = rest.astype(jnp.bfloat16)
    third = (rest - second.astype(jnp.float32)).astype(jnp.bfloat16)
    return first, second, third


def log2(x):
    return jnp.log(x) * log2_e


def paired(me, d, size):
    other, bit = 0, 1
    while bit < size:
        other = other + lax.rem(lax.div(me, bit) + d // bit % 2, 2) * bit
        bit *= 2
    return other


def tree(combine, parts):
    parts = list(parts)
    while len(parts) > 1:
        pairs = [combine(a, b) for a, b in zip(parts[0::2], parts[1::2])]
        parts = pairs + parts[len(parts) // 2 * 2 :]
    return parts[0]


def padded(x):
    return jnp.concatenate([x, jnp.zeros((PAD - F, TILE), jnp.float32)], axis=0)


def kernel(
    wide_size,
    narrow_size,
    cols_ref,
    counts_ref,
    source_hbm,
    target_hbm,
    row_mass_hbm,
    col_mass_hbm,
    row_out_ref,
    col_out_ref,
    gathered,
    target_ref,
    row_mass_ref,
    col_mass_ref,
    right,
    scores,
    one_hot,
    marked,
    source_norm,
    target_norm,
    col_values,
    col_pieces,
    lane_peak,
    lane_mass,
    row_send,
    row_recv,
    slot_lse,
    slot_mass,
    col_peak,
    col_send,
    col_recv,
    load_sem,
    gather_send_sem,
    gather_recv_sem,
    row_send_sem,
    row_recv_sem,
    scatter_send_sem,
    scatter_recv_sem,
    spread_send_sem,
    spread_recv_sem,
):
    wide = lax.axis_index("wide")
    narrow = lax.axis_index("narrow")
    row_count = row_mass_ref.shape[0]
    col_count = col_mass_ref.shape[0]
    shard_tiles = row_count // narrow_size
    piece = col_count // wide_size
    chunk_tiles = col_count // CHUNKS
    chunk_cols = chunk_tiles * TILE

    def wide_peer(d):
        return paired(wide, d, wide_size)

    def narrow_peer(d):
        return paired(narrow, d, narrow_size)

    def at_wide(w):
        return {"wide": w, "narrow": narrow}

    def at_narrow(z):
        return {"wide": wide, "narrow": z}

    def remote(src, dst, send, recv, where):
        return pltpu.make_async_remote_copy(
            src_ref=src,
            dst_ref=dst,
            send_sem=send,
            recv_sem=recv,
            device_id=where,
            device_id_type=pl.DeviceIdType.MESH,
        )

    barrier = pltpu.get_barrier_semaphore()
    for d in range(1, narrow_size):
        pl.semaphore_signal(
            barrier, inc=1, device_id=at_narrow(narrow_peer(d)), device_id_type=pl.DeviceIdType.MESH
        )
    for d in range(1, wide_size):
        pl.semaphore_signal(
            barrier, inc=1, device_id=at_wide(wide_peer(d)), device_id_type=pl.DeviceIdType.MESH
        )
    loads = [pltpu.make_async_copy(source_hbm, gathered.at[narrow], load_sem.at[CHUNKS])]
    for q in range(CHUNKS):
        part = pl.ds(q * chunk_cols, chunk_cols)
        loads.append(
            pltpu.make_async_copy(target_hbm.at[:, part], target_ref.at[:, part], load_sem.at[q])
        )
    loads.append(pltpu.make_async_copy(row_mass_hbm, row_mass_ref, load_sem.at[CHUNKS + 1]))
    loads.append(pltpu.make_async_copy(col_mass_hbm, col_mass_ref, load_sem.at[CHUNKS + 2]))
    for load in loads:
        load.start()
    pl.semaphore_wait(barrier, narrow_size + wide_size - 2)

    def exchange(axis_size, peer, where, src_of, buffer, me, send_sem, recv_sem):
        sends = []
        for d in range(1, axis_size):
            to = peer(d)
            copy = remote(
                src_of(to), buffer.at[me], send_sem.at[d - 1], recv_sem.at[d - 1], where(to)
            )
            copy.start()
            sends.append(copy)

        def arrive(d):
            remote(
                src_of(peer(d)),
                buffer.at[peer(d)],
                send_sem.at[d - 1],
                recv_sem.at[d - 1],
                where(peer(d)),
            ).wait_recv()

        def leave():
            for copy in sends:
                copy.wait_send()

        def finish():
            for d in range(1, axis_size):
                arrive(d)
            leave()

        return finish, arrive, leave

    _, gather_arrive, gather_leave = exchange(
        narrow_size,
        narrow_peer,
        at_narrow,
        lambda to: source_hbm,
        gathered,
        narrow,
        gather_send_sem,
        gather_recv_sem,
    )

    def prepare_target(c, carry):
        x = padded(target_ref[:, pl.ds(pl.multiple_of(c * TILE, TILE), TILE)])
        first, second, third = split_three(x)
        right[c, 0:PAD, :] = first
        right[c, PAD : 2 * PAD, :] = second
        right[c, 2 * PAD : 3 * PAD, :] = third
        norm = jnp.sum(x * x, axis=0, keepdims=True) * norm_scale
        target_norm[pl.ds(c, 1), :] = norm
        return carry

    loads[0].wait()
    for q in range(CHUNKS):
        loads[q + 1].wait()
        lax.fori_loop(q * chunk_tiles, (q + 1) * chunk_tiles, prepare_target, 0)
    col_values[...] = -target_norm[...]
    loads[CHUNKS + 1].wait()
    loads[CHUNKS + 2].wait()

    lane = lax.broadcasted_iota(jnp.int32, (1, TILE), 1)
    row_lane = lax.broadcasted_iota(jnp.int32, (TILE, TILE), 1)
    slab = 8

    def row_tile(r):
        values = [
            jnp.broadcast_to(col_values[pl.ds(cols_ref[k, r], 1), :], (slab, TILE))
            for k in range(K_MAX)
        ]

        def one_group(g, carry):
            for h in range(SLABS):
                rows = pl.ds(pl.multiple_of((g * SLABS + h) * slab, slab), slab)
                s = [scores[r * K_MAX + k, rows, :] + values[k] for k in range(K_MAX)]
                top = tree(jnp.maximum, s)
                lane_mass[r, rows, :] = tree(jnp.add, [jnp.exp2(x - top) for x in s])
                lane_peak[r, rows, :] = top
            return carry

        lax.fori_loop(0, TILE // (slab * SLABS), one_group, 0)

    def row_reduce():
        def one_group(g, columns):
            for j in range(GROUP):
                r = g * GROUP + j
                top = lane_peak[r]
                peak = jnp.max(top, axis=1, keepdims=True)
                mass = jnp.sum(lane_mass[r] * jnp.exp2(top - peak), axis=1, keepdims=True)
                columns = jnp.where(row_lane == r, peak, columns)
                columns = jnp.where(row_lane == r + TILE // 2, mass, columns)
            return columns

        columns = lax.fori_loop(
            0, row_count // GROUP, one_group, jnp.zeros((TILE, TILE), jnp.float32)
        )
        return jnp.transpose(columns)

    def first_tile(r, x):
        source_norm[pl.ds(r, 1), :] = jnp.sum(x * x, axis=0, keepdims=True) * norm_scale
        first, second, third = split_three(x * product_scale)
        first, second, third = [p.astype(jnp.float32) for p in (first, second, third)]
        stacked = jnp.concatenate([first, first, first, second, second, third], axis=0)
        a = jnp.transpose(stacked).astype(jnp.bfloat16)
        marks = []
        for k in range(0, K_MAX, 2):
            pair = []
            for j in (k, k + 1):
                c = cols_ref[j, r]
                alive = j < counts_ref[0, r]
                b = right[c]
                pair.append(jnp.concatenate([b, b[0 : 2 * PAD], b[0:PAD]], axis=0))
                marks.append((lane == jnp.where(alive, c, -1)).astype(jnp.float32))
            product = jnp.dot(
                a, jnp.concatenate(pair, axis=1), preferred_element_type=jnp.float32
            )
            for j in (k, k + 1):
                alive = j < counts_ref[0, r]
                part = product[:, (j - k) * TILE : (j - k + 1) * TILE]
                scores[r * K_MAX + j] = jnp.where(alive, part, very_low)
        marks = jnp.concatenate(marks, axis=0)
        one_hot[pl.ds(pl.multiple_of(r * K_MAX, K_MAX), K_MAX), :] = marks
        unmarked = 1.0 - jnp.sum(marks, axis=0, keepdims=True)
        marked[r] = jnp.concatenate(
            [marks, marks, unmarked, jnp.zeros((2 * K_MAX - 1, TILE), jnp.float32)], axis=0
        ).astype(jnp.bfloat16)
        row_tile(r)

    for d in range(narrow_size):
        if d > 0:
            gather_arrive(d)
        z = narrow_peer(d)

        def one(t, carry):
            x = padded(gathered[z, :, pl.ds(pl.multiple_of(t * TILE, TILE), TILE)])
            first_tile(z * shard_tiles + t, x)
            return carry

        lax.fori_loop(0, shard_tiles, one, 0)
    gather_leave()

    def row_combine(step):
        columns = row_reduce()
        half = TILE // 2
        row_send[step] = columns[0:row_count] + log2(columns[half : half + row_count])
        finish, _, _ = exchange(
            narrow_size,
            narrow_peer,
            at_narrow,
            lambda to: row_send.at[step],
            row_recv.at[step],
            narrow,
            row_send_sem.at[step],
            row_recv_sem.at[step],
        )
        row_recv[step, narrow] = row_send[step]
        finish()
        parts = [row_recv[step, z] for z in range(narrow_size)]
        top = functools.reduce(jnp.maximum, parts)
        total = sum(jnp.exp2(p - top) for p in parts)
        return log2(row_mass_ref[...]) - (top + log2(total))

    def col_pass(step, row_values_ref):
        def one_tile(r, carry):
            values = jnp.transpose(
                jnp.broadcast_to(row_values_ref[pl.ds(r, 1), :], (TILE, TILE))
            )
            results = []
            for k in range(K_MAX):
                s = [
                    scores[r * K_MAX + k, h * slab : (h + 1) * slab, :]
                    + values[h * slab : (h + 1) * slab]
                    for h in range(TILE // slab)
                ]
                top = tree(jnp.maximum, s)
                total = tree(jnp.add, [jnp.exp2(x - top) for x in s])
                peak = jnp.max(top, axis=0, keepdims=True)
                mass = jnp.sum(total * jnp.exp2(top - peak), axis=0, keepdims=True)
                alive = k < counts_ref[0, r]
                results.append((jnp.where(alive, peak, very_low), mass))
            lse = jnp.concatenate([p for p, _ in results], axis=0) + log2(
                jnp.concatenate([m for _, m in results], axis=0)
            )
            slot_lse[pl.ds(pl.multiple_of(r * K_MAX, K_MAX), K_MAX), :] = lse
            coarse = lse.astype(jnp.bfloat16).astype(jnp.float32)
            stack = jnp.concatenate(
                [
                    coarse,
                    lse - coarse,
                    jnp.full((1, TILE), very_low, jnp.float32),
                    jnp.zeros((2 * K_MAX - 1, TILE), jnp.float32),
                ],
                axis=0,
            ).astype(jnp.bfloat16)
            spread = lax.dot_general(
                marked[r],
                stack,
                (((0,), (0,)), ((), ())),
                preferred_element_type=jnp.float32,
            )
            col_peak[...] = jnp.maximum(col_peak[...], spread)
            return carry

        col_peak[...] = jnp.full((col_count, TILE), very_low, jnp.float32)
        lax.fori_loop(0, row_count, one_tile, 0)

        def rescale(r, carry):
            place = pl.ds(pl.multiple_of(r * K_MAX, K_MAX), K_MAX)
            tops = jnp.concatenate(
                [col_peak[pl.ds(cols_ref[k, r], 1), :] for k in range(K_MAX)], axis=0
            )
            slot_mass[place, :] = jnp.exp2(jnp.minimum(slot_lse[place, :] - tops, 1e2))
            return carry

        lax.fori_loop(0, row_count, rescale, 0)
        summed = lax.dot_general(
            one_hot[...],
            slot_mass[...],
            (((0,), (0,)), ((), ())),
            precision=lax.Precision.HIGHEST,
            preferred_element_type=jnp.float32,
        )
        lse = jnp.where(
            summed > 0.0, col_peak[...] + log2(jnp.maximum(summed, 1e-30)), very_low
        )
        for w in range(wide_size):
            col_send[step, w] = lse[w * piece : (w + 1) * piece]
        finish, _, _ = exchange(
            wide_size,
            wide_peer,
            at_wide,
            lambda to: col_send.at[step, to],
            col_recv.at[step],
            wide,
            scatter_send_sem.at[step],
            scatter_recv_sem.at[step],
        )
        col_recv[step, wide] = col_send[step, wide]
        finish()
        parts = [col_recv[step, w] for w in range(wide_size)]
        top = functools.reduce(jnp.maximum, parts)
        total = sum(jnp.exp2(p - top) for p in parts)
        mass = col_mass_ref[pl.ds(pl.multiple_of(wide * piece, piece), piece), :]
        col_pieces[step, wide] = log2(mass) - (top + log2(total))
        finish, _, _ = exchange(
            wide_size,
            wide_peer,
            at_wide,
            lambda to: col_pieces.at[step, wide],
            col_pieces.at[step],
            wide,
            spread_send_sem.at[step],
            spread_recv_sem.at[step],
        )
        finish()
        for w in range(wide_size):
            col_values[w * piece : (w + 1) * piece, :] = col_pieces[step, w]

    def row_pass(r, carry):
        row_tile(r)
        return carry

    for step in range(ITERS):
        if step > 0:
            lax.fori_loop(0, row_count, row_pass, 0)
        row_out_ref[...] = row_combine(step)
        col_pass(step, row_out_ref)
    row_out_ref[...] = potential_scale * (row_out_ref[...] + source_norm[...])
    col_out_ref[...] = potential_scale * (col_values[...] + target_norm[...])


def local(
    wide_size,
    narrow_size,
    source_features,
    target_features,
    source_mass,
    target_mass,
    block_cols,
    block_counts,
):
    row_count = source_mass.shape[0] // TILE
    col_count = target_mass.shape[0] // TILE
    slots = row_count * K_MAX
    piece = col_count // wide_size
    vmem = pl.BlockSpec(memory_space=pltpu.VMEM)
    smem = pl.BlockSpec(memory_space=pltpu.SMEM)
    hbm = pl.BlockSpec(memory_space=pltpu.HBM)
    f32 = jnp.float32
    dma = pltpu.SemaphoreType.DMA
    rows, cols = pl.pallas_call(
        functools.partial(kernel, wide_size, narrow_size),
        out_shape=(
            jax.ShapeDtypeStruct((row_count, TILE), f32),
            jax.ShapeDtypeStruct((col_count, TILE), f32),
        ),
        in_specs=[smem, smem, hbm, hbm, hbm, hbm],
        out_specs=(vmem, vmem),
        scratch_shapes=[
            pltpu.VMEM((narrow_size, F, source_features.shape[1]), f32),
            pltpu.VMEM(target_features.shape, f32),
            pltpu.VMEM((row_count, TILE), f32),
            pltpu.VMEM((col_count, TILE), f32),
            pltpu.VMEM((col_count, 3 * PAD, TILE), jnp.bfloat16),
            pltpu.VMEM((slots, TILE, TILE), f32),
            pltpu.VMEM((slots, col_count), f32),
            pltpu.VMEM((row_count, 4 * K_MAX, col_count), jnp.bfloat16),
            pltpu.VMEM((row_count, TILE), f32),
            pltpu.VMEM((col_count, TILE), f32),
            pltpu.VMEM((col_count, TILE), f32),
            pltpu.VMEM((ITERS, wide_size, piece, TILE), f32),
            pltpu.VMEM((row_count, TILE, TILE), f32),
            pltpu.VMEM((row_count, TILE, TILE), f32),
            pltpu.VMEM((ITERS, row_count, TILE), f32),
            pltpu.VMEM((ITERS, narrow_size, row_count, TILE), f32),
            pltpu.VMEM((slots, TILE), f32),
            pltpu.VMEM((slots, TILE), f32),
            pltpu.VMEM((col_count, TILE), f32),
            pltpu.VMEM((ITERS, wide_size, piece, TILE), f32),
            pltpu.VMEM((ITERS, wide_size, piece, TILE), f32),
            dma((CHUNKS + 3,)),
            dma((narrow_size - 1,)),
            dma((narrow_size - 1,)),
            dma((ITERS, narrow_size - 1)),
            dma((ITERS, narrow_size - 1)),
            dma((ITERS, wide_size - 1)),
            dma((ITERS, wide_size - 1)),
            dma((ITERS, wide_size - 1)),
            dma((ITERS, wide_size - 1)),
        ],
        compiler_params=pltpu.CompilerParams(
            collective_id=0, has_side_effects=True, vmem_limit_bytes=67043328
        ),
    )(
        block_cols.T,
        block_counts.T,
        source_features,
        target_features,
        source_mass.reshape(row_count, TILE),
        target_mass.reshape(col_count, TILE),
    )
    return rows.reshape(-1), cols.reshape(-1)


def solution(mesh):
    in_specs = (
        P(None, ("wide", "narrow")),
        P(None, "narrow"),
        P("wide"),
        P("narrow"),
        P("wide", "narrow"),
        P("wide", "narrow"),
    )
    out_specs = (P("wide"), P("narrow"))
    return jax.shard_map(
        functools.partial(local, mesh.shape["wide"], mesh.shape["narrow"]),
        mesh=mesh,
        in_specs=in_specs,
        out_specs=out_specs,
        check_vma=False,
    )
```

```python
import functools

import jax
import jax.numpy as jnp
from jax import lax
from jax.experimental import pallas as pl
from jax.experimental.pallas import tpu as pltpu
from jax.sharding import PartitionSpec as P

F = 50
TILE = 128
K_MAX = 8
ITERS = 2
PAD = 64
CHUNKS = 4
SLABS = 16
GROUP = 4
HALVES = 2

epsilon = 0.05
very_low = -1e30
log2_e = 1.4426950408889634
product_scale = 2.0 * log2_e / (F * epsilon)
norm_scale = log2_e / (F * epsilon)
potential_scale = epsilon / log2_e


def split_three(x):
    first = x.astype(jnp.bfloat16)
    rest = x - first.astype(jnp.float32)
    second = rest.astype(jnp.bfloat16)
    third = (rest - second.astype(jnp.float32)).astype(jnp.bfloat16)
    return first, second, third


def log2(x):
    return jnp.log(x) * log2_e


def paired(me, d, size):
    other, bit = 0, 1
    while bit < size:
        other = other + lax.rem(lax.div(me, bit) + d // bit % 2, 2) * bit
        bit *= 2
    return other


def tree(combine, parts):
    parts = list(parts)
    while len(parts) > 1:
        pairs = [combine(a, b) for a, b in zip(parts[0::2], parts[1::2])]
        parts = pairs + parts[len(parts) // 2 * 2 :]
    return parts[0]


def padded(x):
    return jnp.concatenate([x, jnp.zeros((PAD - F, TILE), jnp.float32)], axis=0)


def kernel(
    wide_size,
    narrow_size,
    cols_ref,
    counts_ref,
    source_hbm,
    target_hbm,
    row_mass_hbm,
    col_mass_hbm,
    row_out_ref,
    col_out_ref,
    gathered,
    target_ref,
    row_mass_ref,
    col_mass_ref,
    right,
    scores,
    one_hot,
    marked,
    source_norm,
    target_norm,
    col_values,
    col_pieces,
    lane_peak,
    lane_mass,
    row_send,
    row_recv,
    slot_lse,
    slot_mass,
    col_peak,
    col_send,
    col_recv,
    load_sem,
    gather_send_sem,
    gather_recv_sem,
    row_send_sem,
    row_recv_sem,
    scatter_send_sem,
    scatter_recv_sem,
    spread_send_sem,
    spread_recv_sem,
):
    wide = lax.axis_index("wide")
    narrow = lax.axis_index("narrow")
    row_count = row_mass_ref.shape[0]
    col_count = col_mass_ref.shape[0]
    shard_tiles = row_count // narrow_size
    piece = col_count // wide_size
    chunk_tiles = col_count // CHUNKS
    chunk_cols = chunk_tiles * TILE

    def wide_peer(d):
        return paired(wide, d, wide_size)

    def narrow_peer(d):
        return paired(narrow, d, narrow_size)

    def at_wide(w):
        return {"wide": w, "narrow": narrow}

    def at_narrow(z):
        return {"wide": wide, "narrow": z}

    def remote(src, dst, send, recv, where):
        return pltpu.make_async_remote_copy(
            src_ref=src,
            dst_ref=dst,
            send_sem=send,
            recv_sem=recv,
            device_id=where,
            device_id_type=pl.DeviceIdType.MESH,
        )

    barrier = pltpu.get_barrier_semaphore()
    for d in range(1, narrow_size):
        pl.semaphore_signal(
            barrier, inc=1, device_id=at_narrow(narrow_peer(d)), device_id_type=pl.DeviceIdType.MESH
        )
    for d in range(1, wide_size):
        pl.semaphore_signal(
            barrier, inc=1, device_id=at_wide(wide_peer(d)), device_id_type=pl.DeviceIdType.MESH
        )
    loads = [pltpu.make_async_copy(source_hbm, gathered.at[narrow], load_sem.at[CHUNKS])]
    for q in range(CHUNKS):
        part = pl.ds(q * chunk_cols, chunk_cols)
        loads.append(
            pltpu.make_async_copy(target_hbm.at[:, part], target_ref.at[:, part], load_sem.at[q])
        )
    loads.append(pltpu.make_async_copy(row_mass_hbm, row_mass_ref, load_sem.at[CHUNKS + 1]))
    loads.append(pltpu.make_async_copy(col_mass_hbm, col_mass_ref, load_sem.at[CHUNKS + 2]))
    for load in loads:
        load.start()
    pl.semaphore_wait(barrier, narrow_size + wide_size - 2)

    def exchange(axis_size, peer, where, src_of, buffer, me, send_sem, recv_sem):
        sends = []
        for d in range(1, axis_size):
            to = peer(d)
            copy = remote(
                src_of(to), buffer.at[me], send_sem.at[d - 1], recv_sem.at[d - 1], where(to)
            )
            copy.start()
            sends.append(copy)

        def arrive(d):
            remote(
                src_of(peer(d)),
                buffer.at[peer(d)],
                send_sem.at[d - 1],
                recv_sem.at[d - 1],
                where(peer(d)),
            ).wait_recv()

        def leave():
            for copy in sends:
                copy.wait_send()

        def finish():
            for d in range(1, axis_size):
                arrive(d)
            leave()

        return finish, arrive, leave

    _, gather_arrive, gather_leave = exchange(
        narrow_size,
        narrow_peer,
        at_narrow,
        lambda to: source_hbm,
        gathered,
        narrow,
        gather_send_sem,
        gather_recv_sem,
    )

    def prepare_target(c, carry):
        x = padded(target_ref[:, pl.ds(pl.multiple_of(c * TILE, TILE), TILE)])
        first, second, third = split_three(x)
        right[c, 0:PAD, :] = first
        right[c, PAD : 2 * PAD, :] = second
        right[c, 2 * PAD : 3 * PAD, :] = third
        norm = jnp.sum(x * x, axis=0, keepdims=True) * norm_scale
        target_norm[pl.ds(c, 1), :] = norm
        return carry

    loads[0].wait()
    for q in range(CHUNKS):
        loads[q + 1].wait()
        lax.fori_loop(q * chunk_tiles, (q + 1) * chunk_tiles, prepare_target, 0)
    col_values[...] = -target_norm[...]
    loads[CHUNKS + 1].wait()
    loads[CHUNKS + 2].wait()

    lane = lax.broadcasted_iota(jnp.int32, (1, TILE), 1)
    row_lane = lax.broadcasted_iota(jnp.int32, (TILE, TILE), 1)
    slab = 8

    def row_tile(r):
        values = [
            jnp.broadcast_to(col_values[pl.ds(cols_ref[k, r], 1), :], (slab, TILE))
            for k in range(K_MAX)
        ]

        def one_group(g, carry):
            for h in range(SLABS):
                rows = pl.ds(pl.multiple_of((g * SLABS + h) * slab, slab), slab)
                s = [scores[r * K_MAX + k, rows, :] + values[k] for k in range(K_MAX)]
                top = tree(jnp.maximum, s)
                lane_mass[r, rows, :] = tree(jnp.add, [jnp.exp2(x - top) for x in s])
                lane_peak[r, rows, :] = top
            return carry

        lax.fori_loop(0, TILE // (slab * SLABS), one_group, 0)

    half_count = row_count // HALVES

    def row_reduce(part):
        def one_group(g, columns):
            for j in range(GROUP):
                r = part * half_count + g * GROUP + j
                top = lane_peak[r]
                peak = jnp.max(top, axis=1, keepdims=True)
                mass = jnp.sum(lane_mass[r] * jnp.exp2(top - peak), axis=1, keepdims=True)
                columns = jnp.where(row_lane == r, peak, columns)
                columns = jnp.where(row_lane == r + TILE // 2, mass, columns)
            return columns

        columns = lax.fori_loop(
            0, half_count // GROUP, one_group, jnp.zeros((TILE, TILE), jnp.float32)
        )
        return jnp.transpose(columns)

    def first_tile(r, x):
        source_norm[pl.ds(r, 1), :] = jnp.sum(x * x, axis=0, keepdims=True) * norm_scale
        first, second, third = split_three(x * product_scale)
        first, second, third = [p.astype(jnp.float32) for p in (first, second, third)]
        stacked = jnp.concatenate([first, first, first, second, second, third], axis=0)
        a = jnp.transpose(stacked).astype(jnp.bfloat16)
        marks = []
        for k in range(0, K_MAX, 2):
            pair = []
            for j in (k, k + 1):
                c = cols_ref[j, r]
                alive = j < counts_ref[0, r]
                b = right[c]
                pair.append(jnp.concatenate([b, b[0 : 2 * PAD], b[0:PAD]], axis=0))
                marks.append((lane == jnp.where(alive, c, -1)).astype(jnp.float32))
            product = jnp.dot(
                a, jnp.concatenate(pair, axis=1), preferred_element_type=jnp.float32
            )
            for j in (k, k + 1):
                alive = j < counts_ref[0, r]
                part = product[:, (j - k) * TILE : (j - k + 1) * TILE]
                scores[r * K_MAX + j] = jnp.where(alive, part, very_low)
        marks = jnp.concatenate(marks, axis=0)
        one_hot[pl.ds(pl.multiple_of(r * K_MAX, K_MAX), K_MAX), :] = marks
        unmarked = 1.0 - jnp.sum(marks, axis=0, keepdims=True)
        marked[r] = jnp.concatenate(
            [marks, marks, unmarked, jnp.zeros((2 * K_MAX - 1, TILE), jnp.float32)], axis=0
        ).astype(jnp.bfloat16)
        row_tile(r)

    for d in range(narrow_size):
        if d > 0:
            gather_arrive(d)
        z = narrow_peer(d)

        def one(t, carry):
            x = padded(gathered[z, :, pl.ds(pl.multiple_of(t * TILE, TILE), TILE)])
            first_tile(z * shard_tiles + t, x)
            return carry

        lax.fori_loop(0, shard_tiles, one, 0)
    gather_leave()

    def row_share(step, part):
        columns = row_reduce(part)
        first, half = part * half_count, TILE // 2
        row_send[step, part] = columns[first : first + half_count] + log2(
            columns[half + first : half + first + half_count]
        )
        finish, _, _ = exchange(
            narrow_size,
            narrow_peer,
            at_narrow,
            lambda to: row_send.at[step, part],
            row_recv.at[step, part],
            narrow,
            row_send_sem.at[step, part],
            row_recv_sem.at[step, part],
        )
        row_recv[step, part, narrow] = row_send[step, part]
        return finish

    def row_combine(step, part, finish):
        finish()
        parts = [row_recv[step, part, z] for z in range(narrow_size)]
        top = functools.reduce(jnp.maximum, parts)
        total = sum(jnp.exp2(p - top) for p in parts)
        rows = slice(part * half_count, (part + 1) * half_count)
        row_out_ref[rows, :] = log2(row_mass_ref[rows, :]) - (top + log2(total))

    def col_pass(step, row_values_ref, finishes):
        def one_tile(r, carry):
            values = jnp.transpose(
                jnp.broadcast_to(row_values_ref[pl.ds(r, 1), :], (TILE, TILE))
            )
            results = []
            for k in range(K_MAX):
                s = [
                    scores[r * K_MAX + k, h * slab : (h + 1) * slab, :]
                    + values[h * slab : (h + 1) * slab]
                    for h in range(TILE // slab)
                ]
                top = tree(jnp.maximum, s)
                total = tree(jnp.add, [jnp.exp2(x - top) for x in s])
                peak = jnp.max(top, axis=0, keepdims=True)
                mass = jnp.sum(total * jnp.exp2(top - peak), axis=0, keepdims=True)
                alive = k < counts_ref[0, r]
                results.append((jnp.where(alive, peak, very_low), mass))
            lse = jnp.concatenate([p for p, _ in results], axis=0) + log2(
                jnp.concatenate([m for _, m in results], axis=0)
            )
            slot_lse[pl.ds(pl.multiple_of(r * K_MAX, K_MAX), K_MAX), :] = lse
            coarse = lse.astype(jnp.bfloat16).astype(jnp.float32)
            stack = jnp.concatenate(
                [
                    coarse,
                    lse - coarse,
                    jnp.full((1, TILE), very_low, jnp.float32),
                    jnp.zeros((2 * K_MAX - 1, TILE), jnp.float32),
                ],
                axis=0,
            ).astype(jnp.bfloat16)
            spread = lax.dot_general(
                marked[r],
                stack,
                (((0,), (0,)), ((), ())),
                preferred_element_type=jnp.float32,
            )
            col_peak[...] = jnp.maximum(col_peak[...], spread)
            return carry

        col_peak[...] = jnp.full((col_count, TILE), very_low, jnp.float32)
        for part in range(HALVES):
            row_combine(step, part, finishes[part])
            lax.fori_loop(part * half_count, (part + 1) * half_count, one_tile, 0)

        def rescale(r, carry):
            place = pl.ds(pl.multiple_of(r * K_MAX, K_MAX), K_MAX)
            tops = jnp.concatenate(
                [col_peak[pl.ds(cols_ref[k, r], 1), :] for k in range(K_MAX)], axis=0
            )
            slot_mass[place, :] = jnp.exp2(jnp.minimum(slot_lse[place, :] - tops, 1e2))
            return carry

        lax.fori_loop(0, row_count, rescale, 0)
        summed = lax.dot_general(
            one_hot[...],
            slot_mass[...],
            (((0,), (0,)), ((), ())),
            precision=lax.Precision.HIGHEST,
            preferred_element_type=jnp.float32,
        )
        lse = jnp.where(
            summed > 0.0, col_peak[...] + log2(jnp.maximum(summed, 1e-30)), very_low
        )
        for w in range(wide_size):
            col_send[step, w] = lse[w * piece : (w + 1) * piece]
        finish, _, _ = exchange(
            wide_size,
            wide_peer,
            at_wide,
            lambda to: col_send.at[step, to],
            col_recv.at[step],
            wide,
            scatter_send_sem.at[step],
            scatter_recv_sem.at[step],
        )
        col_recv[step, wide] = col_send[step, wide]
        finish()
        parts = [col_recv[step, w] for w in range(wide_size)]
        top = functools.reduce(jnp.maximum, parts)
        total = sum(jnp.exp2(p - top) for p in parts)
        mass = col_mass_ref[pl.ds(pl.multiple_of(wide * piece, piece), piece), :]
        col_pieces[step, wide] = log2(mass) - (top + log2(total))
        finish, _, _ = exchange(
            wide_size,
            wide_peer,
            at_wide,
            lambda to: col_pieces.at[step, wide],
            col_pieces.at[step],
            wide,
            spread_send_sem.at[step],
            spread_recv_sem.at[step],
        )
        finish()
        for w in range(wide_size):
            col_values[w * piece : (w + 1) * piece, :] = col_pieces[step, w]

    def row_pass(r, carry):
        row_tile(r)
        return carry

    for step in range(ITERS):
        finishes = []
        for part in range(HALVES):
            if step > 0:
                lax.fori_loop(part * half_count, (part + 1) * half_count, row_pass, 0)
            finishes.append(row_share(step, part))
        col_pass(step, row_out_ref, finishes)
    row_out_ref[...] = potential_scale * (row_out_ref[...] + source_norm[...])
    col_out_ref[...] = potential_scale * (col_values[...] + target_norm[...])


def local(
    wide_size,
    narrow_size,
    source_features,
    target_features,
    source_mass,
    target_mass,
    block_cols,
    block_counts,
):
    row_count = source_mass.shape[0] // TILE
    col_count = target_mass.shape[0] // TILE
    slots = row_count * K_MAX
    piece = col_count // wide_size
    vmem = pl.BlockSpec(memory_space=pltpu.VMEM)
    smem = pl.BlockSpec(memory_space=pltpu.SMEM)
    hbm = pl.BlockSpec(memory_space=pltpu.HBM)
    f32 = jnp.float32
    dma = pltpu.SemaphoreType.DMA
    rows, cols = pl.pallas_call(
        functools.partial(kernel, wide_size, narrow_size),
        out_shape=(
            jax.ShapeDtypeStruct((row_count, TILE), f32),
            jax.ShapeDtypeStruct((col_count, TILE), f32),
        ),
        in_specs=[smem, smem, hbm, hbm, hbm, hbm],
        out_specs=(vmem, vmem),
        scratch_shapes=[
            pltpu.VMEM((narrow_size, F, source_features.shape[1]), f32),
            pltpu.VMEM(target_features.shape, f32),
            pltpu.VMEM((row_count, TILE), f32),
            pltpu.VMEM((col_count, TILE), f32),
            pltpu.VMEM((col_count, 3 * PAD, TILE), jnp.bfloat16),
            pltpu.VMEM((slots, TILE, TILE), f32),
            pltpu.VMEM((slots, col_count), f32),
            pltpu.VMEM((row_count, 4 * K_MAX, col_count), jnp.bfloat16),
            pltpu.VMEM((row_count, TILE), f32),
            pltpu.VMEM((col_count, TILE), f32),
            pltpu.VMEM((col_count, TILE), f32),
            pltpu.VMEM((ITERS, wide_size, piece, TILE), f32),
            pltpu.VMEM((row_count, TILE, TILE), f32),
            pltpu.VMEM((row_count, TILE, TILE), f32),
            pltpu.VMEM((ITERS, HALVES, row_count // HALVES, TILE), f32),
            pltpu.VMEM((ITERS, HALVES, narrow_size, row_count // HALVES, TILE), f32),
            pltpu.VMEM((slots, TILE), f32),
            pltpu.VMEM((slots, TILE), f32),
            pltpu.VMEM((col_count, TILE), f32),
            pltpu.VMEM((ITERS, wide_size, piece, TILE), f32),
            pltpu.VMEM((ITERS, wide_size, piece, TILE), f32),
            dma((CHUNKS + 3,)),
            dma((narrow_size - 1,)),
            dma((narrow_size - 1,)),
            dma((ITERS, HALVES, narrow_size - 1)),
            dma((ITERS, HALVES, narrow_size - 1)),
            dma((ITERS, wide_size - 1)),
            dma((ITERS, wide_size - 1)),
            dma((ITERS, wide_size - 1)),
            dma((ITERS, wide_size - 1)),
        ],
        compiler_params=pltpu.CompilerParams(
            collective_id=0, has_side_effects=True, vmem_limit_bytes=67043328
        ),
    )(
        block_cols.T,
        block_counts.T,
        source_features,
        target_features,
        source_mass.reshape(row_count, TILE),
        target_mass.reshape(col_count, TILE),
    )
    return rows.reshape(-1), cols.reshape(-1)


def solution(mesh):
    in_specs = (
        P(None, ("wide", "narrow")),
        P(None, "narrow"),
        P("wide"),
        P("narrow"),
        P("wide", "narrow"),
        P("wide", "narrow"),
    )
    out_specs = (P("wide"), P("narrow"))
    return jax.shard_map(
        functools.partial(local, mesh.shape["wide"], mesh.shape["narrow"]),
        mesh=mesh,
        in_specs=in_specs,
        out_specs=out_specs,
        check_vma=False,
    )
```
